768 devices in a mesh: xs: 16 (over y, z_hi), ys: 48 (over z_lo, x, core).
Axes of the slice: x: 4, y: 8, z: 12 (z_hi: 2, z_lo: 6; z = z_hi * 6 + z_lo), core: 2. Of those that a mesh axis runs over, the one named last changes fastest.
Arguments:
- fields: float32 [6, 16, 512, 6144], P(None, None, 'xs', 'ys'), may hold values from -6 to 6
- permittivity: float32 [16, 512, 6144], P(None, 'xs', 'ys'), may hold values from 1 to 12
- adj_values: float32 [73728, 128], P(('xs', 'ys')), may hold values from -6 to 6
- adj_owner: int32 [73728, 1], P(('xs', 'ys')), may hold values from 0 to 47; in each aligned block of 96 rows (0 to 95, 96 to 191, ...) at most 4 rows name the same one
- adj_row: int32 [73728], P(('xs', 'ys')), may hold values from 0 to 31
- angle_wave: int32 [128], replicated, may hold values from 0 to 4999
Outputs:
- new_fields: float32 [6, 16, 512, 6144], P(None, None, 'xs', 'ys')
- far_field: float32 [128, 2, 4, 6144], P('xs', None, None, 'ys')
The draws below stay inside these ranges and needn't reach their ends.
Inputs may be any that keep to these rules, and one draw needn't show every extreme that they name: `adj_owner`: among the 96 rows of one device no ys index is named more than 4 times.
All inputs are finite; a program needn't handle non-finite values.
Results may differ from the reference program's by a relative error of at most 0.000071.
Values sent between devices are 32-bit elements; how exact they have to be, the bound alone decides.
A program may use at most 64 MiB of HBM per device.

```python
import math
import jax
import jax.numpy as jnp
import numpy as np
from jax import lax

CX = 32
CY = 128
NZ = 16
STEPS = 3
CAP = 4
GRID_X = 5000
X0 = 2000
ZS = 8
ADJ_DEV = 96
NX = 512
NY = 6144
KA = 128
BLOCKS = 73728
N_YS = 48


def place_ends(array, rng, smallest, top_value):
    extent = array.shape
    index_at = [jax.random.randint(jax.random.fold_in(rng, axis), (), 0, extent[axis]) for axis in range(len(extent))]
    array = array.at[tuple(index_at)].set(smallest)
    longest = extent.index(max(extent))
    index_at[longest] = (index_at[longest] + 1) % extent[longest]
    return array.at[tuple(index_at)].set(top_value)


def level_of(own_key, dims, cuts, smallest, largest):
    loudness = 1.0
    for dim, shards_of in cuts:
        heights = jax.random.uniform(jax.random.fold_in(jax.random.fold_in(own_key, 6), dim), (shards_of,), jnp.float32, smallest / len(cuts), largest / len(cuts))
        loudness = loudness * jnp.repeat(jnp.exp(heights), dims[dim] // shards_of).reshape((-1,) + (1,) * (len(dims) - 1 - dim))
    return loudness


def deal_out(stream_key, own, number, rows, count, top, most, slope):
    ranking = jax.random.permutation(stream_key, count)
    heavy_load, ordinary = load_shares(count, rows * top, most, slope, True), load_shares(count, rows * top, most, slope, False)
    places = jnp.arange(count)

    def named(tallies, rotation):
        used = int((tallies > 0).sum())
        fixed = max(1, used // 4)
        moved = fixed + (places - fixed + rotation * (used - fixed)) % max(1, count - fixed)
        return jnp.zeros((count,), jnp.int32).at[ranking[jnp.where(places < fixed, places, moved)]].set(jnp.asarray(tallies, jnp.int32))

    tallies = jnp.where(number % 4 == 0, named(heavy_load, number // 4), named(ordinary, number - number // 4 - 1))
    mixed = jax.random.permutation(jax.random.fold_in(own, 3), count)
    giver, receiver = mixed[0:count // 2 * 2:2], mixed[1:count // 2 * 2:2]
    room = jnp.minimum(tallies[giver] - 1, most - tallies[receiver]) // 2
    room = jnp.where((giver == ranking[0]) | (receiver == ranking[0]) | (tallies[receiver] == 0), 0, jnp.maximum(room, 0))
    moved = jax.random.randint(jax.random.fold_in(own, 4), (count // 2,), 0, 1 << 20) % (room + 1)
    tallies = tallies.at[giver].add(-moved).at[receiver].add(moved)
    labels = jnp.searchsorted(jnp.cumsum(tallies), jnp.arange(rows * top), side="right").astype(jnp.int32)
    listing = labels.reshape(top, rows).T
    listing = listing[jax.random.permutation(jax.random.fold_in(own, 1), rows)]
    rotation = jax.random.randint(jax.random.fold_in(own, 2), (rows, 1), 0, top)
    return jnp.take_along_axis(listing, (jnp.arange(top)[None, :] + rotation) % top, axis=1)


def load_shares(amount, total, bound, slope, full):
    loads = [(1 << 20) // math.isqrt(grade ** slope) + 1 for grade in range(1, amount + 1)]
    largest = bound if full else min(bound, max(-(-total // amount), total * loads[0] // sum(loads)))
    least = 1 if total - largest >= amount - 1 else 0
    given, rest = [largest] + [least] * (amount - 1), total - largest - least * (amount - 1)
    while rest > 0:
        free = [i for i in range(1, amount) if given[i] < largest] or [i for i in range(1, amount) if given[i] < bound]
        mass, remaining = sum([loads[i] for i in free]), rest
        for i in free:
            extra = min(bound - given[i], max(1, remaining * loads[i] // mass), rest)
            given[i] = given[i] + extra
            rest = rest - extra
    return np.array(given)


def bell_draw(key, shape, deviation, bound, cuts=(), kind=jnp.bfloat16):
    loudness = level_of(key, shape, cuts, -0.22, 0.18) if cuts else 1.0
    drawn = jax.random.normal(key, shape, jnp.float32) * deviation * loudness
    return jnp.minimum(jnp.maximum(drawn, -bound), bound).astype(kind)


def setup_inputs(seed: int = 0) -> dict:
    splits = jax.random.split(jax.random.key(seed), 7)
    fields = bell_draw(splits[0], (6, NZ, NX, NY), 1.0, 6.0, ((2, 16), (3, 48)), jnp.float32)
    permittivity = jnp.clip(jnp.exp(math.log(12.0) - 2.4849066 * jax.random.uniform(splits[1], (NZ, NX, NY), jnp.float32) ** level_of(splits[1], (NZ, NX, NY), ((1, 16), (2, 48)), -0.2, 0.2)), 1.0, 12.0)
    adj_values = bell_draw(splits[2], (BLOCKS, CY), 1.0, 6.0, ((0, 768),), jnp.float32)
    adj_owner_keys = jax.random.split(jax.random.fold_in(splits[3], 1), BLOCKS // ADJ_DEV)
    adj_owner_turns = jax.random.permutation(jax.random.fold_in(splits[3], 3), BLOCKS // ADJ_DEV)
    adj_owner = jax.vmap(lambda own, number: deal_out(jax.random.fold_in(splits[3], 2), own, number, ADJ_DEV, N_YS, 1, CAP, 2))(adj_owner_keys, adj_owner_turns).reshape((BLOCKS, 1))
    adj_row = place_ends(jax.random.randint(splits[4], (BLOCKS,), 0, CX), jax.random.fold_in(splits[4], 1), 0, CX - 1).astype(jnp.int32)
    angle_wave = place_ends(jax.random.randint(splits[5], (KA,), 0, GRID_X), jax.random.fold_in(splits[5], 1), 0, GRID_X - 1).astype(jnp.int32)
    return {"fields": fields, "permittivity": permittivity, "adj_values": adj_values, "adj_owner": adj_owner, "adj_row": adj_row, "angle_wave": angle_wave}


time_step = 0.5

def along_next(inner, edge, axis):
    return jnp.concatenate([lax.slice_in_dim(inner, 1, inner.shape[axis], axis=axis), edge], axis)

def along_prev(inner, edge, axis):
    return jnp.concatenate([edge, lax.slice_in_dim(inner, 0, inner.shape[axis] - 1, axis=axis)], axis)

def advance(fields, coeffs, source, next_x, next_y, prev_x, prev_y):
    elec = [fields[0], fields[1], fields[2]]
    magn = [fields[3], fields[4], fields[5]]
    zero_layer = jnp.zeros((1,) + elec[0].shape[1:], jnp.float32)
    edge_x = next_x(jnp.stack([elec[1][:, 0, :], elec[2][:, 0, :]]))
    edge_y = next_y(jnp.stack([elec[0][:, :, 0], elec[2][:, :, 0]]))
    ey_xnext = along_next(elec[1], edge_x[0][:, None, :], 1)
    ez_xnext = along_next(elec[2], edge_x[1][:, None, :], 1)
    ex_ynext = along_next(elec[0], edge_y[0][:, :, None], 2)
    ez_ynext = along_next(elec[2], edge_y[1][:, :, None], 2)
    ex_znext = along_next(elec[0], zero_layer, 0)
    ey_znext = along_next(elec[1], zero_layer, 0)
    hx_new = magn[0] - time_step * (ez_ynext - elec[2] - (ey_znext - elec[1]))
    hy_new = magn[1] - time_step * (ex_znext - elec[0] - (ez_xnext - elec[2]))
    hz_new = magn[2] - time_step * (ey_xnext - elec[1] - (ex_ynext - elec[0]))
    back_x = prev_x(jnp.stack([hy_new[:, -1, :], hz_new[:, -1, :]]))
    back_y = prev_y(jnp.stack([hx_new[:, :, -1], hz_new[:, :, -1]]))
    hy_xprev = along_prev(hy_new, back_x[0][:, None, :], 1)
    hz_xprev = along_prev(hz_new, back_x[1][:, None, :], 1)
    hx_yprev = along_prev(hx_new, back_y[0][:, :, None], 2)
    hz_yprev = along_prev(hz_new, back_y[1][:, :, None], 2)
    hx_zprev = along_prev(hx_new, zero_layer, 0)
    hy_zprev = along_prev(hy_new, zero_layer, 0)
    ex_new = elec[0] + coeffs * (hz_new - hz_yprev - (hy_new - hy_zprev))
    ey_new = elec[1] + coeffs * (hx_new - hx_zprev - (hz_new - hz_xprev))
    ez_new = elec[2] + coeffs * (hy_new - hy_xprev - (hx_new - hx_yprev) - source)
    return jnp.stack([ex_new, ey_new, ez_new, hx_new, hy_new, hz_new])

def spectrum(tile, angles, first_x):
    positions = X0 + first_x + jnp.arange(tile.shape[1], dtype=jnp.int32)
    phase = angles[:, None] * positions[None, :] % GRID_X
    angle = phase.astype(jnp.float32) * (2.0 * math.pi / GRID_X)
    cosine = jnp.cos(angle)
    sine = -jnp.sin(angle)
    real_part = jnp.einsum('ax,cxy->acy', cosine, tile, precision=lax.Precision.HIGHEST)
    imag_part = jnp.einsum('ax,cxy->acy', sine, tile, precision=lax.Precision.HIGHEST)
    return jnp.stack([real_part, imag_part], axis=1)

def zero_rim(plane):
    return jnp.zeros_like(plane)

def reference(fields, permittivity, adj_values, adj_owner, adj_row, angle_wave):
    width_x = fields.shape[2]
    width_y = fields.shape[3]
    device = jnp.arange(adj_values.shape[0], dtype=jnp.int32) // ADJ_DEV
    row_x = device // N_YS * CX + adj_row
    columns = adj_owner[:, 0][:, None] * CY + jnp.arange(CY, dtype=jnp.int32)[None, :]
    rows_full = jnp.broadcast_to(row_x[:, None], columns.shape)
    current = jnp.zeros((width_x, width_y), jnp.float32).at[rows_full, columns].add(adj_values)
    coeffs = time_step / permittivity
    layer_mask = (jnp.arange(NZ, dtype=jnp.int32) == ZS).astype(jnp.float32)[:, None, None]
    source = layer_mask * current[None]
    for iteration in range(STEPS):
        fields = advance(fields, coeffs, source, zero_rim, zero_rim, zero_rim, zero_rim)
    tile = jnp.stack([-fields[4][ZS], fields[3][ZS], fields[1][ZS], -fields[0][ZS]])
    far_field = spectrum(tile, angle_wave, 0) / math.sqrt(width_x)
    return (fields, far_field)
```

```python
import math

import jax
import jax.numpy as jnp
from jax import lax
from jax.experimental import pallas as pl
from jax.experimental.pallas import tpu as pltpu
from jax.sharding import PartitionSpec as P

GRID_X = 5000
X0 = 2000
ZS = 8
DT = 0.5
NXS = 16
NYS = 48
NZ = 16
CX = 32
RX = 40
LANES = 128
HI = lax.Precision.HIGHEST

FROM_PREV = (
    [(k, r) for k in (0, 1, 2, 4, 5) for r in (29, 30, 31)]
    + [(3, 30), (3, 31)]
    + [(6, 30), (6, 31)]
)
FROM_NEXT = (
    [(k, r) for k in (1, 2) for r in (0, 1, 2)]
    + [(k, r) for k in (0, 3, 4, 5) for r in (0, 1)]
    + [(6, 0), (6, 1)]
)
NLO = len(FROM_PREV)
NHI = len(FROM_NEXT)
EARLY = 5


def rows_of(boxes):
    found, at = [], 0
    for comps, r, first, count in boxes:
        for k in comps:
            found.append((k, r, first, count, at))
            at += count
    return found, at


ALL = tuple(range(7))
TILE_PREV, TLO = rows_of(((ALL, 31, 6, 5), (ALL, 30, 7, 3), ((0, 1, 5), 29, 8, 1)))
TILE_NEXT, THI = rows_of(((ALL, 0, 5, 6), (ALL, 1, 6, 4), ((1, 2), 2, 7, 2)))


def iota(shape, axis):
    return lax.broadcasted_iota(jnp.int32, shape, axis)


def half_h(e, h, dt, ops):
    ex, ey, ez = e
    hx, hy, hz = h
    xn, yn, zn = ops
    hx2 = hx - dt * ((yn(ez, 1) - ez) - (zn(ey, 1) - ey))
    hy2 = hy - dt * ((zn(ex, 0) - ex) - (xn(ez) - ez))
    hz2 = hz - dt * ((xn(ey) - ey) - (yn(ex, 0) - ex))
    return hx2, hy2, hz2


def half_e(e, h, c, source, ops):
    ex, ey, ez = e
    hx, hy, hz = h
    xp, yp, zp = ops
    ex2 = ex + c * ((hz - yp(hz, 1)) - (hy - zp(hy, 1)))
    ey2 = ey + c * ((hx - zp(hx, 0)) - (hz - xp(hz)))
    ez2 = ez + c * ((hy - xp(hy)) - (hx - yp(hx, 0)) - source)
    return ex2, ey2, ez2


def kernel(
    fields_ref, perm_ref, adj_ref, owner_ref, row_ref, angle_ref,
    newf_ref, far_ref,
    fld, tmp, strip, own_p, own_p4, in_p, in_p4, ye, yh, dtf, dts,
    send_lo, send_hi, recv_lo, recv_hi, tsend_lo, tsend_hi, trecv_lo, trecv_hi,
    outbox, inbox, cur, cur_p, in_sx, in_sp, in_sd, src_s,
    tiles, weights, zsend, zrecv,
    load_sem, a_send, a_recv, x_send, x_recv, p_send, p_recv, p4_send, p4_recv,
    s_send, s_recv, t_send, t_recv, z_send, z_recv,
):
    mx = lax.axis_index("xs")
    my = lax.axis_index("ys")
    xn_dev = lax.rem(mx + 1, NXS)
    xp_dev = lax.rem(mx + NXS - 1, NXS)
    yn_dev = lax.rem(my + 1, NYS)
    yp_dev = lax.rem(my + NYS - 1, NYS)
    ring = mx // 2
    zh = lax.rem(mx, 2)
    partner = ring * 2 + (1 - zh)
    m_xlo = jnp.where(mx == 0, 0.0, 1.0)
    m_xhi = jnp.where(mx == NXS - 1, 0.0, 1.0)
    m_ylo = jnp.where(my == 0, 0.0, 1.0)
    m_yhi = jnp.where(my == NYS - 1, 0.0, 1.0)

    def remote(src, dst, ssem, rsem, dev):
        return pltpu.make_async_remote_copy(
            src_ref=src, dst_ref=dst, send_sem=ssem, recv_sem=rsem,
            device_id=dev, device_id_type=pl.DeviceIdType.MESH,
        )

    inbox[...] = jnp.zeros(inbox.shape, jnp.float32)
    bar = pltpu.get_barrier_semaphore()

    def greet(dev):
        pl.semaphore_signal(bar, inc=1, device_id=dev, device_id_type=pl.DeviceIdType.MESH)

    near = [
        (xn_dev, my), (xp_dev, my),
        (xn_dev, yn_dev), (xn_dev, yp_dev), (xp_dev, yn_dev), (xp_dev, yp_dev),
    ] + [(lax.rem(ring + d, 8) * 2 + zh, my) for d in range(1, 8)]
    for dev in near:
        greet(dev)

    @pl.loop(1, NYS)
    def _(d):
        greet((mx, lax.rem(my + d, NYS)))

    load_f = pltpu.make_async_copy(
        fields_ref, fld.at[pl.ds(0, 6), pl.ds(1, NZ), pl.ds(0, CX), :], load_sem.at[0]
    )
    load_c = pltpu.make_async_copy(
        perm_ref, fld.at[6, pl.ds(1, NZ), pl.ds(0, CX), :], load_sem.at[1]
    )
    load_f.start()
    load_c.start()

    n_adj = adj_ref.shape[0]
    own_row = owner_ref[...].astype(jnp.float32)
    ii = iota((n_adj, n_adj), 0)
    jj = iota((n_adj, n_adj), 1)
    own_b = jnp.broadcast_to(own_row, (n_adj, n_adj))
    row_b = jnp.broadcast_to(row_ref[...].astype(jnp.float32), (n_adj, n_adj))
    own_col = jnp.sum(jnp.where(ii == jj, own_b, 0.0), axis=1, keepdims=True)
    row_col = jnp.sum(jnp.where(ii == jj, row_b, 0.0), axis=1, keepdims=True)
    same = own_col == own_b
    rank_row = jnp.sum(jnp.where(same & (ii < jj), 1.0, 0.0), axis=0, keepdims=True)
    rank_col = jnp.sum(jnp.where(same & (jj < ii), 1.0, 0.0), axis=1, keepdims=True)
    place = iota((NYS * 8, n_adj), 0).astype(jnp.float32)
    pick_val = jnp.where(place == own_row * 8.0 + rank_row, 1.0, 0.0)
    pick_row = jnp.where(place == own_row * 8.0 + 4.0, 1.0, 0.0)
    lane_f = iota((n_adj, LANES), 1).astype(jnp.float32)
    base = (lax.rem(my, 16) * 8).astype(jnp.float32)
    row_at = jnp.where(lane_f == base + rank_col, row_col + 1.0, 0.0)
    out = jnp.dot(pick_val, adj_ref[...], precision=HI, preferred_element_type=jnp.float32)
    out = out + jnp.dot(pick_row, row_at, precision=HI, preferred_element_type=jnp.float32)
    outbox[...] = out.reshape(NYS, 8, LANES)

    lane = iota((8, LANES), 1)
    for k in range(7):
        for z in range(NZ + 2):
            fld[k, z, pl.ds(CX, 8), :] = jnp.zeros((8, LANES), jnp.float32)
        for z in (0, NZ + 1):
            fld[k, z, pl.ds(0, CX), :] = jnp.zeros((CX, LANES), jnp.float32)
    for k in (3, 4):
        tmp[k, 5, :, :] = jnp.zeros((RX, LANES), jnp.float32)
    r40 = iota((RX, LANES), 0)
    row_m = jnp.where(
        r40 < CX, 1.0, jnp.where(r40 < CX + 3, m_xhi, jnp.where(r40 >= RX - 3, m_xlo, 0.0))
    )
    dtf[...] = DT * row_m
    slot40 = iota((RX, LANES), 1) & 7
    dts[0] = DT * row_m * jnp.where(slot40 < 3, m_ylo, jnp.where(slot40 < 6, 1.0, 0.0))
    dts[1] = DT * row_m * jnp.where(slot40 < 3, 1.0, jnp.where(slot40 < 6, m_yhi, 0.0))

    load_f.wait()
    load_c.wait()

    @pl.loop(1, NZ + 1)
    def _(z):
        fld[6, z, pl.ds(0, CX), :] = DT / fld[6, z, pl.ds(0, CX), :]

    flat = fld.reshape(7 * (NZ + 2) * RX, LANES)

    def rows_at(k, z, r, n):
        return pl.ds((k * (NZ + 2) + z + 1) * RX + r, n, stride=RX)

    def pack_x(send, rows, early, early_rows):
        for k, r, z, n, at in early_rows:
            early[pl.ds(at, n), :] = flat[rows_at(k, z, r, n), :]
        for i, (k, r) in enumerate(rows):
            send[i, :, :] = flat[rows_at(k, 0, r, NZ), :]

    pack_x(send_lo, FROM_PREV, tsend_lo, TILE_PREV)
    pack_x(send_hi, FROM_NEXT, tsend_hi, TILE_NEXT)

    def pack_strip(load, n):
        lanes = iota((n, LANES), 1)
        total = jnp.zeros((n, LANES), jnp.float32)
        for z in range(NZ):
            turned = pltpu.roll(load(z), 8 * z + 3, 1)
            total = jnp.where((lanes >> 3) == z, turned, total)
        return jnp.where((lanes & 7) < 6, total, 0.0)

    @pl.loop(0, 7)
    def _(k):
        own_p[k, :, :] = pack_strip(lambda z: fld[k, z + 1, pl.ds(0, CX), :], CX)

    r32 = iota((32, LANES), 0)
    owner_xs = jnp.where(r32 < 16, ring * 2 + zh, ring * 2 + (1 - zh))
    a_index = owner_xs * 8 + ((r32 & 15) >> 1)
    angle_row = jnp.broadcast_to(angle_ref[...].astype(jnp.float32), (32, LANES))
    wave = jnp.sum(
        jnp.where(iota((32, LANES), 1) == a_index, angle_row, 0.0), axis=1, keepdims=True
    )
    col = iota((32, 8 * CX), 1)
    x_pos = ((col >> 5) * 2 + zh) * CX + (col & 31) + X0
    prod = wave * x_pos.astype(jnp.float32)
    turn = prod - jnp.floor(prod * (1.0 / GRID_X)) * float(GRID_X)
    turn = jnp.where(turn < 0.0, turn + float(GRID_X), turn)
    turn = jnp.where(turn >= float(GRID_X), turn - float(GRID_X), turn)
    quad = jnp.floor(turn * (4.0 / GRID_X) + 0.5)
    th = (turn - quad * (GRID_X / 4.0)) * (2.0 * math.pi / GRID_X)
    t2 = th * th
    sn = th * (1.0 + t2 * (-1.0 / 6 + t2 * (1.0 / 120 + t2 * (-1.0 / 5040 + t2 * (1.0 / 362880)))))
    cs = 1.0 + t2 * (-0.5 + t2 * (1.0 / 24 + t2 * (-1.0 / 720 + t2 * (1.0 / 40320 - t2 * (1.0 / 3628800)))))
    odd = (quad == 1.0) | (quad == 3.0)
    c_abs = jnp.where(odd, sn, cs)
    s_abs = jnp.where(odd, cs, sn)
    cosine = jnp.where((quad == 1.0) | (quad == 2.0), -c_abs, c_abs)
    sine = jnp.where((quad == 2.0) | (quad == 3.0), -s_abs, s_abs)
    scale = 1.0 / math.sqrt(NXS * CX)
    is_re = (iota((32, 8 * CX), 0) & 1) == 0
    weights[...] = jnp.where(is_re, cosine, -sine) * scale

    pl.semaphore_wait(bar, len(near) + NYS - 1)

    def a_copy(d):
        to = lax.rem(my + d, NYS)
        return remote(
            outbox.at[to, pl.ds(0, 5), :], inbox.at[my, pl.ds(0, 5), :],
            a_send.at[d], a_recv.at[my], (mx, to),
        )

    @pl.loop(1, NYS)
    def _(d):
        a_copy(d).start()

    def x_copies(i, part, count):
        lo, hi = pl.ds(part, count or NLO - part), pl.ds(part, count or NHI - part)
        return [
            remote(send_lo.at[lo], recv_lo.at[lo], x_send.at[i, 0], x_recv.at[i, 0], (xn_dev, my)),
            remote(send_hi.at[hi], recv_hi.at[hi], x_send.at[i, 1], x_recv.at[i, 1], (xp_dev, my)),
        ]

    x_first = [
        remote(tsend_lo, trecv_lo, x_send.at[0, 0], x_recv.at[0, 0], (xn_dev, my)),
        remote(tsend_hi, trecv_hi, x_send.at[0, 1], x_recv.at[0, 1], (xp_dev, my)),
    ]
    x_early = x_copies(1, 0, EARLY)
    for c in x_first:
        c.start()
    p_copies = [
        remote(own_p, in_p.at[0], p_send.at[0], p_recv.at[0], (mx, yn_dev)),
        remote(own_p, in_p.at[1], p_send.at[1], p_recv.at[1], (mx, yp_dev)),
    ]
    for c in p_copies + x_early:
        c.start()

    inbox[my] = outbox[my]

    @pl.loop(1, NYS)
    def _(d):
        frm = lax.rem(my + d, NYS)
        remote(
            outbox.at[frm, pl.ds(0, 5), :], inbox.at[frm, pl.ds(0, 5), :],
            a_send.at[d], a_recv.at[frm], (mx, frm),
        ).wait_recv()

    current = jnp.zeros((CX, LANES), jnp.float32)
    x_id = (iota((CX, LANES), 0) + 1).astype(jnp.float32)
    for q in range(3):
        block = inbox[pl.ds(16 * q, 16), :, :]
        ids = jnp.sum(inbox[pl.ds(16 * q, 16), 4, :], axis=0, keepdims=True)
        landing = jnp.where(x_id == ids, 1.0, 0.0)
        current = current + jnp.dot(
            landing, block.reshape(16 * 8, LANES), precision=HI, preferred_element_type=jnp.float32
        )
    cur[pl.ds(0, CX), :] = current

    def pack_s(v):
        lanes = iota(v.shape, 1)
        inside = (lanes >= 8 * ZS) & (lanes < 8 * ZS + 6)
        return jnp.where(inside, pltpu.roll(v, 8 * ZS + 3, 1), 0.0)

    cur_p[pl.ds(0, CX), :] = pack_s(current)
    lo8 = pl.ds(0, 8)
    hi8 = pl.ds(CX - 8, 8)
    s_copies = [
        remote(cur.at[hi8, :], in_sx.at[0], s_send.at[0], s_recv.at[0], (xn_dev, my)),
        remote(cur.at[lo8, :], in_sx.at[1], s_send.at[1], s_recv.at[1], (xp_dev, my)),
        remote(cur_p.at[hi8, :], in_sd.at[0, 0], s_send.at[2], s_recv.at[2], (xn_dev, yn_dev)),
        remote(cur_p.at[hi8, :], in_sd.at[0, 1], s_send.at[3], s_recv.at[3], (xn_dev, yp_dev)),
        remote(cur_p.at[lo8, :], in_sd.at[1, 0], s_send.at[4], s_recv.at[4], (xp_dev, yn_dev)),
        remote(cur_p.at[lo8, :], in_sd.at[1, 1], s_send.at[5], s_recv.at[5], (xp_dev, yp_dev)),
        remote(cur_p.at[pl.ds(0, CX), :], in_sp.at[0], s_send.at[6], s_recv.at[6], (mx, yn_dev)),
        remote(cur_p.at[pl.ds(0, CX), :], in_sp.at[1], s_send.at[7], s_recv.at[7], (mx, yp_dev)),
    ]
    for c in s_copies:
        c.start()
    x_second = x_copies(2, EARLY, 0)
    for c in x_second:
        c.start()

    def unpack_x(recv, rows, early, early_rows, base, mask):
        for k, r, z, n, at in early_rows:
            flat[rows_at(k, z, r + base, n), :] = early[pl.ds(at, n), :] * mask
        for i, (k, r) in enumerate(rows):
            flat[rows_at(k, 0, r + base, NZ), :] = recv[i, :, :] * mask

    def p4_copies(part):
        return [
            remote(own_p4.at[part], in_p4.at[part, 0], p4_send.at[part, 0], p4_recv.at[part, 0], (mx, yn_dev)),
            remote(own_p4.at[part], in_p4.at[part, 1], p4_send.at[part, 1], p4_recv.at[part, 1], (mx, yp_dev)),
        ]

    def halo_in(part, copies):
        for c in copies:
            c.wait_recv()
        if part == 0:
            unpack_x(None, (), trecv_lo, TILE_PREV, 8, m_xlo)
            unpack_x(None, (), trecv_hi, TILE_NEXT, CX, m_xhi)
        else:
            unpack_x(recv_lo, FROM_PREV, None, (), 8, m_xlo)
            unpack_x(recv_hi, FROM_NEXT, None, (), CX, m_xhi)

        @pl.loop(0, 7)
        def _(k):
            own_p4[part, k, :, :] = pack_strip(lambda z: fld[k, z + 1, pl.ds(CX, 8), :], 8)

        sent = p4_copies(part)
        for c in sent:
            c.start()
        return sent

    def build_strips(part):
        @pl.loop(0, 7)
        def _(k):
            for rows, own, got in (
                (pl.ds(0, CX), own_p[k], (in_p[0, k], in_p[1, k])),
                (pl.ds(CX, 8), own_p4[part, k], (in_p4[part, 0, k], in_p4[part, 1, k])),
            ):
                low = (iota(own.shape, 1) & 7) < 3
                strip[0, k, rows, :] = jnp.where(low, got[0] * m_ylo, own)
                strip[1, k, rows, :] = jnp.where(low, own, got[1] * m_yhi)

    lane40 = iota((RX, LANES), 1)

    def x_next(v):
        return pltpu.roll(v, RX - 1, 0)

    def x_prev(v):
        return pltpu.roll(v, 1, 0)

    def strips_run():
        def zn(v, _):
            return jnp.where(lane40 < 8 * (NZ - 1), pltpu.roll(v, LANES - 8, 1), 0.0)

        def zp(v, _):
            return jnp.where(lane40 >= 8, pltpu.roll(v, 8, 1), 0.0)

        def yn(v, _):
            return pltpu.roll(v, LANES - 1, 1)

        def yp(v, _):
            return pltpu.roll(v, 1, 1)

        for step in range(3):
            for side in range(2):
                e = [strip[side, k] for k in range(3)]
                if side == 1:
                    ye[step, 0, :, :] = e[0]
                    ye[step, 1, :, :] = e[2]
                    if step == 2:
                        continue
                h = [strip[side, k] for k in range(3, 6)]
                h = half_h(e, h, dts[side], (x_next, yn, zn))
                if side == 0:
                    yh[step, 0, :, :] = h[0]
                    yh[step, 1, :, :] = h[2]
                    if step == 2:
                        continue
                e = half_e(e, h, strip[side, 6], src_s[side], (x_prev, yp, zp))
                for k in range(3):
                    strip[side, k, :, :] = e[k]
                    strip[side, 3 + k, :, :] = h[k]

    def sweep(step, src, dst, first, last):
        @pl.loop(first, last + 1)
        def _(z):
            sh_e = lax.rem(124 - 8 * (z - 1) + 128, 128)
            sh_h = lax.rem(126 - 8 * (z - 1) + 128, 128)
            dt = dtf[...]
            e = [src[k, z] for k in range(3)]
            h = [src[k, z] for k in range(3, 6)]

            def yn(v, i):
                edge = pltpu.roll(ye[step, i], sh_e, 1)
                return jnp.where(lane40 == LANES - 1, edge, pltpu.roll(v, LANES - 1, 1))

            def zn(v, i):
                return src[i, z + 1]

            def yp(v, i):
                edge = pltpu.roll(yh[step, i], sh_h, 1)
                return jnp.where(lane40 == 0, edge, pltpu.roll(v, 1, 1))

            def zp(v, i):
                return dst[3 + i, z - 1]

            h = half_h(e, h, dt, (x_next, yn, zn))
            on = jnp.where(z == ZS + 1, 1.0, 0.0)
            e = half_e(e, h, fld[6, z], cur[...] * on, (x_prev, yp, zp))
            for k in range(3):
                dst[k, z] = e[k]
                dst[3 + k, z] = h[k]

    p4_first = halo_in(0, x_first)
    for c in p_copies:
        c.wait_recv()
    for c in p4_first:
        c.wait_recv()
    build_strips(0)
    for c in s_copies:
        c.wait_recv()
    r8 = iota((8, LANES), 0)

    def tile4(lo, hi):
        return jnp.where(r8 < 3, hi * m_xhi, jnp.where(r8 >= 5, lo * m_xlo, 0.0))

    cur4 = tile4(in_sx[0], in_sx[1])
    cur[pl.ds(CX, 8), :] = cur4
    own4 = pack_s(cur4)
    low32 = (iota((CX, LANES), 1) & 7) < 3
    low8 = (lane & 7) < 3
    own32 = cur_p[pl.ds(0, CX), :]
    src_s[0, pl.ds(0, CX), :] = jnp.where(low32, in_sp[0] * m_ylo, own32)
    src_s[1, pl.ds(0, CX), :] = jnp.where(low32, own32, in_sp[1] * m_yhi)
    src_s[0, pl.ds(CX, 8), :] = jnp.where(low8, tile4(in_sd[0, 0], in_sd[1, 0]) * m_ylo, own4)
    src_s[1, pl.ds(CX, 8), :] = jnp.where(low8, own4, tile4(in_sd[0, 1], in_sd[1, 1]) * m_yhi)

    strips_run()
    sweep(0, fld, tmp, 6, 11)
    sweep(1, tmp, tmp, 7, 10)
    sweep(2, tmp, tmp, 8, 9)
    own_x = pl.ds(0, CX)
    mine = pl.ds(ring * CX, CX)
    tiles[0, mine, :] = -tmp[4, ZS + 1, own_x, :]
    tiles[1, mine, :] = tmp[3, ZS + 1, own_x, :]
    tiles[2, mine, :] = tmp[1, ZS + 1, own_x, :]
    tiles[3, mine, :] = -tmp[0, ZS + 1, own_x, :]

    def t_copy(d, c, whose):
        at = pl.ds(pl.multiple_of(whose * CX, CX), CX)
        to = lax.rem(ring + d, 8) * 2 + zh
        return remote(
            tiles.at[c, at, :], tiles.at[c, at, :],
            t_send.at[d - 1, c], t_recv.at[d - 1, c], (to, my),
        )

    for c in range(4):
        for d in (4, 3, 5, 2, 6, 1, 7):
            t_copy(d, c, ring).start()

    p4_second = halo_in(1, x_early + x_second)

    z_copies = []
    for c in range(4):
        for d in range(1, 8):
            t_copy(d, c, lax.rem(ring + 8 - d, 8)).wait_recv()
        zsend[c, :, :] = jnp.dot(
            weights[...], tiles[c], precision=HI, preferred_element_type=jnp.float32
        )
        copy = remote(zsend.at[c, pl.ds(16, 16), :], zrecv.at[c], z_send.at[c], z_recv.at[c], (partner, my))
        copy.start()
        z_copies.append(copy)

    for c in p4_second:
        c.wait_recv()
    build_strips(1)
    strips_run()
    for step in range(3):
        sweep(step, fld, fld, 1, NZ)
    store = pltpu.make_async_copy(
        fld.at[pl.ds(0, 6), pl.ds(1, NZ), pl.ds(0, CX), :], newf_ref, load_sem.at[2]
    )
    store.start()

    for c in range(4):
        z_copies[c].wait_recv()
        far_ref[pl.ds(c, 16, stride=4), :] = zsend[c, pl.ds(0, 16), :] + zrecv[c]

    @pl.loop(1, NYS)
    def _(d):
        a_copy(d).wait_send()

    for c in x_first + x_early + x_second + p_copies + p4_first + p4_second + s_copies + z_copies:
        c.wait_send()
    for c in range(4):
        for d in range(1, 8):
            t_copy(d, c, ring).wait_send()
    store.wait()


def on_device(fields, permittivity, adj_values, adj_owner, adj_row, angle_wave):
    n_adj = adj_values.shape[0]
    f32 = jnp.float32
    vmem = lambda *shape: pltpu.VMEM(shape, f32)
    dma = pltpu.SemaphoreType.DMA
    whole = pl.BlockSpec(memory_space=pltpu.VMEM)
    anywhere = pl.BlockSpec(memory_space=pl.ANY)
    new_fields, far = pl.pallas_call(
        kernel,
        out_shape=(
            jax.ShapeDtypeStruct(fields.shape, f32),
            jax.ShapeDtypeStruct((64, LANES), f32),
        ),
        in_specs=[anywhere, anywhere, whole, whole, whole, whole],
        out_specs=(anywhere, whole),
        scratch_shapes=[
            vmem(7, NZ + 2, RX, LANES),
            vmem(6, NZ + 2, RX, LANES),
            vmem(2, 7, RX, LANES),
            vmem(7, CX, LANES),
            vmem(2, 7, 8, LANES),
            vmem(2, 7, CX, LANES),
            vmem(2, 2, 7, 8, LANES),
            vmem(3, 2, RX, LANES),
            vmem(3, 2, RX, LANES),
            vmem(RX, LANES),
            vmem(2, RX, LANES),
            vmem(NLO, NZ, LANES),
            vmem(NHI, NZ, LANES),
            vmem(NLO, NZ, LANES),
            vmem(NHI, NZ, LANES),
            vmem(TLO, LANES),
            vmem(THI, LANES),
            vmem(TLO, LANES),
            vmem(THI, LANES),
            vmem(NYS, 8, LANES),
            vmem(NYS, 8, LANES),
            vmem(RX, LANES),
            vmem(RX, LANES),
            vmem(2, 8, LANES),
            vmem(2, CX, LANES),
            vmem(2, 2, 8, LANES),
            vmem(2, RX, LANES),
            vmem(4, 8 * CX, LANES),
            vmem(32, 8 * CX),
            vmem(4, 32, LANES),
            vmem(4, 16, LANES),
            dma((3,)),
            dma((NYS,)),
            dma((NYS,)),
            dma((3, 2)),
            dma((3, 2)),
            dma((2,)),
            dma((2,)),
            dma((2, 2)),
            dma((2, 2)),
            dma((8,)),
            dma((8,)),
            dma((7, 4)),
            dma((7, 4)),
            dma((4,)),
            dma((4,)),
        ],
        compiler_params=pltpu.CompilerParams(collective_id=1, has_side_effects=True),
        name="fdtd_far_field",
    )(
        fields,
        permittivity,
        adj_values,
        adj_owner.reshape(1, n_adj),
        adj_row.reshape(1, n_adj),
        angle_wave.reshape(1, angle_wave.shape[0]),
    )
    return new_fields, far.reshape(8, 2, 4, LANES)


def solution(mesh):
    placed = (
        P(None, None, "xs", "ys"),
        P(None, "xs", "ys"),
        P(("xs", "ys"), None),
        P(("xs", "ys"), None),
        P(("xs", "ys")),
        P(),
    )
    return jax.shard_map(
        on_device,
        mesh=mesh,
        in_specs=placed,
        out_specs=(P(None, None, "xs", "ys"), P("xs", None, None, "ys")),
        check_vma=False,
    )
```

```python
import math

import jax
import jax.numpy as jnp
from jax import lax
from jax.experimental import pallas as pl
from jax.experimental.pallas import tpu as pltpu
from jax.sharding import PartitionSpec as P

GRID_X = 5000
X0 = 2000
ZS = 8
DT = 0.5
NXS = 16
NYS = 48
NZ = 16
CX = 32
RX = 40
LANES = 128
HI = lax.Precision.HIGHEST

FROM_PREV = (
    [(k, r) for k in (0, 1, 2, 4, 5) for r in (29, 30, 31)]
    + [(3, 30), (3, 31)]
    + [(6, 30), (6, 31)]
)
FROM_NEXT = (
    [(k, r) for k in (1, 2) for r in (0, 1, 2)]
    + [(k, r) for k in (0, 3, 4, 5) for r in (0, 1)]
    + [(6, 0), (6, 1)]
)
ALL = tuple(range(7))
EARLY = 2


def split_halo(slabs, boxes):
    inner = {(k, r): (z, n) for comps, r, z, n in boxes for k in comps}
    tile = [(k, r, z, n) for (k, r), (z, n) in inner.items()]
    outer = ([], [])
    for i, (k, r) in enumerate(slabs):
        z, n = inner.get((k, r), (NZ, 0))
        outer[i >= EARLY].append((k, r, 0, z))
        if z + n < NZ:
            outer[i >= EARLY].append((k, r, z + n, NZ - z - n))
    parts = []
    for entries in (tile, *outer):
        placed, at = [], 0
        for k, r, z, n in entries:
            placed.append((k, r, z, n, at))
            at += n
        parts.append((placed, at))
    return parts


PARTS_LO = split_halo(FROM_PREV, ((ALL, 31, 6, 5), (ALL, 30, 7, 3), ((0, 1, 5), 29, 8, 1)))
PARTS_HI = split_halo(FROM_NEXT, ((ALL, 0, 5, 6), (ALL, 1, 6, 4), ((1, 2), 2, 7, 2)))


def iota(shape, axis):
    return lax.broadcasted_iota(jnp.int32, shape, axis)


def half_h(e, h, dt, ops):
    ex, ey, ez = e
    hx, hy, hz = h
    xn, yn, zn = ops
    hx2 = hx - dt * ((yn(ez, 1) - ez) - (zn(ey, 1) - ey))
    hy2 = hy - dt * ((zn(ex, 0) - ex) - (xn(ez) - ez))
    hz2 = hz - dt * ((xn(ey) - ey) - (yn(ex, 0) - ex))
    return hx2, hy2, hz2


def half_e(e, h, c, source, ops):
    ex, ey, ez = e
    hx, hy, hz = h
    xp, yp, zp = ops
    ex2 = ex + c * ((hz - yp(hz, 1)) - (hy - zp(hy, 1)))
    ey2 = ey + c * ((hx - zp(hx, 0)) - (hz - xp(hz)))
    ez2 = ez + c * ((hy - xp(hy)) - (hx - yp(hx, 0)) - source)
    return ex2, ey2, ez2


def kernel(
    fields_ref, perm_ref, adj_ref, owner_ref, row_ref, angle_ref,
    newf_ref, far_ref,
    fld, tmp, strip, own_p, own_p4, in_p, in_p4, ye, yh, dtf, dts,
    send_lo0, send_lo1, send_lo2, send_hi0, send_hi1, send_hi2,
    recv_lo0, recv_lo1, recv_lo2, recv_hi0, recv_hi1, recv_hi2,
    outbox, inbox, cur, cur_p, in_sx, in_sp, in_sd, src_s,
    tiles, weights, zsend, zrecv,
    load_sem, a_send, a_recv, x_send, x_recv, p_send, p_recv, p4_send, p4_recv,
    s_send, s_recv, t_send, t_recv, z_send, z_recv,
):
    send_lo, send_hi = (send_lo0, send_lo1, send_lo2), (send_hi0, send_hi1, send_hi2)
    recv_lo, recv_hi = (recv_lo0, recv_lo1, recv_lo2), (recv_hi0, recv_hi1, recv_hi2)
    mx = lax.axis_index("xs")
    my = lax.axis_index("ys")
    xn_dev = lax.rem(mx + 1, NXS)
    xp_dev = lax.rem(mx + NXS - 1, NXS)
    yn_dev = lax.rem(my + 1, NYS)
    yp_dev = lax.rem(my + NYS - 1, NYS)
    ring = mx // 2
    zh = lax.rem(mx, 2)
    partner = ring * 2 + (1 - zh)
    m_xlo = jnp.where(mx == 0, 0.0, 1.0)
    m_xhi = jnp.where(mx == NXS - 1, 0.0, 1.0)
    m_ylo = jnp.where(my == 0, 0.0, 1.0)
    m_yhi = jnp.where(my == NYS - 1, 0.0, 1.0)

    def remote(src, dst, ssem, rsem, dev):
        return pltpu.make_async_remote_copy(
            src_ref=src, dst_ref=dst, send_sem=ssem, recv_sem=rsem,
            device_id=dev, device_id_type=pl.DeviceIdType.MESH,
        )

    inbox[...] = jnp.zeros(inbox.shape, jnp.float32)
    bar = pltpu.get_barrier_semaphore()

    def greet(dev):
        pl.semaphore_signal(bar, inc=1, device_id=dev, device_id_type=pl.DeviceIdType.MESH)

    near = [
        (xn_dev, my), (xp_dev, my),
        (xn_dev, yn_dev), (xn_dev, yp_dev), (xp_dev, yn_dev), (xp_dev, yp_dev),
    ] + [(lax.rem(ring + d, 8) * 2 + zh, my) for d in range(1, 8)]
    for dev in near:
        greet(dev)

    @pl.loop(1, NYS)
    def _(d):
        greet((mx, lax.rem(my + d, NYS)))

    load_f = pltpu.make_async_copy(
        fields_ref, fld.at[pl.ds(0, 6), pl.ds(1, NZ), pl.ds(0, CX), :], load_sem.at[0]
    )
    load_c = pltpu.make_async_copy(
        perm_ref, fld.at[6, pl.ds(1, NZ), pl.ds(0, CX), :], load_sem.at[1]
    )
    load_f.start()
    load_c.start()

    n_adj = adj_ref.shape[0]
    own_row = owner_ref[...].astype(jnp.float32)
    ii = iota((n_adj, n_adj), 0)
    jj = iota((n_adj, n_adj), 1)
    own_b = jnp.broadcast_to(own_row, (n_adj, n_adj))
    row_b = jnp.broadcast_to(row_ref[...].astype(jnp.float32), (n_adj, n_adj))
    own_col = jnp.sum(jnp.where(ii == jj, own_b, 0.0), axis=1, keepdims=True)
    row_col = jnp.sum(jnp.where(ii == jj, row_b, 0.0), axis=1, keepdims=True)
    same = own_col == own_b
    rank_row = jnp.sum(jnp.where(same & (ii < jj), 1.0, 0.0), axis=0, keepdims=True)
    rank_col = jnp.sum(jnp.where(same & (jj < ii), 1.0, 0.0), axis=1, keepdims=True)
    place = iota((NYS * 8, n_adj), 0).astype(jnp.float32)
    pick_val = jnp.where(place == own_row * 8.0 + rank_row, 1.0, 0.0)
    pick_row = jnp.where(place == own_row * 8.0 + 4.0, 1.0, 0.0)
    lane_f = iota((n_adj, LANES), 1).astype(jnp.float32)
    base = (lax.rem(my, 16) * 8).astype(jnp.float32)
    row_at = jnp.where(lane_f == base + rank_col, row_col + 1.0, 0.0)
    out = jnp.dot(pick_val, adj_ref[...], precision=HI, preferred_element_type=jnp.float32)
    out = out + jnp.dot(pick_row, row_at, precision=HI, preferred_element_type=jnp.float32)
    outbox[...] = out.reshape(NYS, 8, LANES)

    lane = iota((8, LANES), 1)
    for k in range(7):
        for z in range(NZ + 2):
            fld[k, z, pl.ds(CX, 8), :] = jnp.zeros((8, LANES), jnp.float32)
        for z in (0, NZ + 1):
            fld[k, z, pl.ds(0, CX), :] = jnp.zeros((CX, LANES), jnp.float32)
    for k, z in ((3, 5), (4, 5), (3, 0), (4, 0), (0, NZ + 1), (1, NZ + 1)):
        tmp[k, z, :, :] = jnp.zeros((RX, LANES), jnp.float32)
    r40 = iota((RX, LANES), 0)
    row_m = jnp.where(
        r40 < CX, 1.0, jnp.where(r40 < CX + 3, m_xhi, jnp.where(r40 >= RX - 3, m_xlo, 0.0))
    )
    dtf[...] = DT * row_m
    slot40 = iota((RX, LANES), 1) & 7
    dts[0] = DT * row_m * jnp.where(slot40 < 3, m_ylo, jnp.where(slot40 < 6, 1.0, 0.0))
    dts[1] = DT * row_m * jnp.where(slot40 < 3, 1.0, jnp.where(slot40 < 6, m_yhi, 0.0))

    load_f.wait()
    load_c.wait()

    @pl.loop(1, NZ + 1)
    def _(z):
        fld[6, z, pl.ds(0, CX), :] = DT / fld[6, z, pl.ds(0, CX), :]

    flat = fld.reshape(7 * (NZ + 2) * RX, LANES)

    def rows_at(k, z, r, n):
        return pl.ds((k * (NZ + 2) + z + 1) * RX + r, n, stride=RX)

    for sends, parts in ((send_lo, PARTS_LO), (send_hi, PARTS_HI)):
        for send, (entries, _) in zip(sends, parts):
            for k, r, z, n, at in entries:
                send[pl.ds(at, n), :] = flat[rows_at(k, z, r, n), :]

    def pack_strip(load, n):
        lanes = iota((n, LANES), 1)
        total = jnp.zeros((n, LANES), jnp.float32)
        for z in range(NZ):
            turned = pltpu.roll(load(z), 8 * z + 3, 1)
            total = jnp.where((lanes >> 3) == z, turned, total)
        return jnp.where((lanes & 7) < 6, total, 0.0)

    @pl.loop(0, 7)
    def _(k):
        own_p[k, :, :] = pack_strip(lambda z: fld[k, z + 1, pl.ds(0, CX), :], CX)

    r32 = iota((32, LANES), 0)
    owner_xs = jnp.where(r32 < 16, ring * 2 + zh, ring * 2 + (1 - zh))
    a_index = owner_xs * 8 + ((r32 & 15) >> 1)
    angle_row = jnp.broadcast_to(angle_ref[...].astype(jnp.float32), (32, LANES))
    wave = jnp.sum(
        jnp.where(iota((32, LANES), 1) == a_index, angle_row, 0.0), axis=1, keepdims=True
    )
    col = iota((32, 8 * CX), 1)
    x_pos = ((col >> 5) * 2 + zh) * CX + (col & 31) + X0
    prod = wave * x_pos.astype(jnp.float32)
    turn = prod - jnp.floor(prod * (1.0 / GRID_X)) * float(GRID_X)
    turn = jnp.where(turn < 0.0, turn + float(GRID_X), turn)
    turn = jnp.where(turn >= float(GRID_X), turn - float(GRID_X), turn)
    quad = jnp.floor(turn * (4.0 / GRID_X) + 0.5)
    th = (turn - quad * (GRID_X / 4.0)) * (2.0 * math.pi / GRID_X)
    t2 = th * th
    sn = th * (1.0 + t2 * (-1.0 / 6 + t2 * (1.0 / 120 + t2 * (-1.0 / 5040 + t2 * (1.0 / 362880)))))
    cs = 1.0 + t2 * (-0.5 + t2 * (1.0 / 24 + t2 * (-1.0 / 720 + t2 * (1.0 / 40320 - t2 * (1.0 / 3628800)))))
    odd = (quad == 1.0) | (quad == 3.0)
    c_abs = jnp.where(odd, sn, cs)
    s_abs = jnp.where(odd, cs, sn)
    cosine = jnp.where((quad == 1.0) | (quad == 2.0), -c_abs, c_abs)
    sine = jnp.where((quad == 2.0) | (quad == 3.0), -s_abs, s_abs)
    scale = 1.0 / math.sqrt(NXS * CX)
    is_re = (iota((32, 8 * CX), 0) & 1) == 0
    weights[...] = jnp.where(is_re, cosine, -sine) * scale

    pl.semaphore_wait(bar, len(near) + NYS - 1)

    def a_copy(d):
        to = lax.rem(my + d, NYS)
        return remote(
            outbox.at[to, pl.ds(0, 5), :], inbox.at[my, pl.ds(0, 5), :],
            a_send.at[d], a_recv.at[my], (mx, to),
        )

    @pl.loop(1, NYS)
    def _(d):
        a_copy(d).start()

    def x_copies(i):
        return [
            remote(send_lo[i], recv_lo[i], x_send.at[i, 0], x_recv.at[i, 0], (xn_dev, my)),
            remote(send_hi[i], recv_hi[i], x_send.at[i, 1], x_recv.at[i, 1], (xp_dev, my)),
        ]

    x_first, x_early, x_second = x_copies(0), x_copies(1), x_copies(2)
    for c in x_first:
        c.start()
    p_copies = [
        remote(own_p, in_p.at[0], p_send.at[0], p_recv.at[0], (mx, yn_dev)),
        remote(own_p, in_p.at[1], p_send.at[1], p_recv.at[1], (mx, yp_dev)),
    ]
    for c in p_copies + x_early:
        c.start()

    inbox[my] = outbox[my]

    @pl.loop(1, NYS)
    def _(d):
        frm = lax.rem(my + d, NYS)
        remote(
            outbox.at[frm, pl.ds(0, 5), :], inbox.at[frm, pl.ds(0, 5), :],
            a_send.at[d], a_recv.at[frm], (mx, frm),
        ).wait_recv()

    current = jnp.zeros((CX, LANES), jnp.float32)
    x_id = (iota((CX, LANES), 0) + 1).astype(jnp.float32)
    for q in range(3):
        block = inbox[pl.ds(16 * q, 16), :, :]
        ids = jnp.sum(inbox[pl.ds(16 * q, 16), 4, :], axis=0, keepdims=True)
        landing = jnp.where(x_id == ids, 1.0, 0.0)
        current = current + jnp.dot(
            landing, block.reshape(16 * 8, LANES), precision=HI, preferred_element_type=jnp.float32
        )
    cur[pl.ds(0, CX), :] = current

    def pack_s(v):
        lanes = iota(v.shape, 1)
        inside = (lanes >= 8 * ZS) & (lanes < 8 * ZS + 6)
        return jnp.where(inside, pltpu.roll(v, 8 * ZS + 3, 1), 0.0)

    cur_p[pl.ds(0, CX), :] = pack_s(current)
    lo8 = pl.ds(0, 8)
    hi8 = pl.ds(CX - 8, 8)
    s_copies = [
        remote(cur.at[hi8, :], in_sx.at[0], s_send.at[0], s_recv.at[0], (xn_dev, my)),
        remote(cur.at[lo8, :], in_sx.at[1], s_send.at[1], s_recv.at[1], (xp_dev, my)),
        remote(cur_p.at[hi8, :], in_sd.at[0, 0], s_send.at[2], s_recv.at[2], (xn_dev, yn_dev)),
        remote(cur_p.at[hi8, :], in_sd.at[0, 1], s_send.at[3], s_recv.at[3], (xn_dev, yp_dev)),
        remote(cur_p.at[lo8, :], in_sd.at[1, 0], s_send.at[4], s_recv.at[4], (xp_dev, yn_dev)),
        remote(cur_p.at[lo8, :], in_sd.at[1, 1], s_send.at[5], s_recv.at[5], (xp_dev, yp_dev)),
        remote(cur_p.at[pl.ds(0, CX), :], in_sp.at[0], s_send.at[6], s_recv.at[6], (mx, yn_dev)),
        remote(cur_p.at[pl.ds(0, CX), :], in_sp.at[1], s_send.at[7], s_recv.at[7], (mx, yp_dev)),
    ]
    for c in s_copies:
        c.start()

    def unpack_x(i):
        for recv, parts, base, mask in (
            (recv_lo, PARTS_LO, 8, m_xlo), (recv_hi, PARTS_HI, CX, m_xhi)
        ):
            for k, r, z, n, at in parts[i][0]:
                flat[rows_at(k, z, r + base, n), :] = recv[i][pl.ds(at, n), :] * mask

    def p4_copies(part):
        return [
            remote(own_p4.at[part], in_p4.at[part, 0], p4_send.at[part, 0], p4_recv.at[part, 0], (mx, yn_dev)),
            remote(own_p4.at[part], in_p4.at[part, 1], p4_send.at[part, 1], p4_recv.at[part, 1], (mx, yp_dev)),
        ]

    def halo_in(part, copies):
        for c in copies:
            c.wait_recv()
        for i in (0,) if part == 0 else (1, 2):
            unpack_x(i)

        @pl.loop(0, 7)
        def _(k):
            own_p4[part, k, :, :] = pack_strip(lambda z: fld[k, z + 1, pl.ds(CX, 8), :], 8)

        sent = p4_copies(part)
        for c in sent:
            c.start()
        return sent

    def build_strips(part):
        @pl.loop(0, 7)
        def _(k):
            for rows, own, got in (
                (pl.ds(0, CX), own_p[k], (in_p[0, k], in_p[1, k])),
                (pl.ds(CX, 8), own_p4[part, k], (in_p4[part, 0, k], in_p4[part, 1, k])),
            ):
                low = (iota(own.shape, 1) & 7) < 3
                strip[0, k, rows, :] = jnp.where(low, got[0] * m_ylo, own)
                strip[1, k, rows, :] = jnp.where(low, own, got[1] * m_yhi)

    lane40 = iota((RX, LANES), 1)

    def x_next(v):
        return pltpu.roll(v, RX - 1, 0)

    def x_prev(v):
        return pltpu.roll(v, 1, 0)

    def strips_run():
        def zn(v, _):
            return jnp.where(lane40 < 8 * (NZ - 1), pltpu.roll(v, LANES - 8, 1), 0.0)

        def zp(v, _):
            return jnp.where(lane40 >= 8, pltpu.roll(v, 8, 1), 0.0)

        def yn(v, _):
            return pltpu.roll(v, LANES - 1, 1)

        def yp(v, _):
            return pltpu.roll(v, 1, 1)

        for step in range(3):
            for side in range(2):
                e = [strip[side, k] for k in range(3)]
                if side == 1:
                    ye[step, 0, :, :] = e[0]
                    ye[step, 1, :, :] = e[2]
                    if step == 2:
                        continue
                h = [strip[side, k] for k in range(3, 6)]
                h = half_h(e, h, dts[side], (x_next, yn, zn))
                if side == 0:
                    yh[step, 0, :, :] = h[0]
                    yh[step, 1, :, :] = h[2]
                    if step == 2:
                        continue
                e = half_e(e, h, strip[side, 6], src_s[side], (x_prev, yp, zp))
                for k in range(3):
                    strip[side, k, :, :] = e[k]
                    strip[side, 3 + k, :, :] = h[k]

    def sweep(step, src, dst, first, last, rows, keep=None):
        height = sum(n for _, n in rows)
        lanes = iota((height, LANES), 1)

        def take(ref, *at):
            got = [ref[(*at, pl.ds(r, n), slice(None))] for r, n in rows]
            return got[0] if len(got) == 1 else jnp.concatenate(got, axis=0)

        def x_next(v):
            return pltpu.roll(v, height - 1, 0)

        def x_prev(v):
            return pltpu.roll(v, 1, 0)

        @pl.loop(first, last + 1)
        def _(z):
            sh_e = lax.rem(124 - 8 * (z - 1) + 128, 128)
            sh_h = lax.rem(126 - 8 * (z - 1) + 128, 128)
            dt = take(dtf)
            e = [take(src, k, z) for k in range(3)]
            h = [take(src, k, z) for k in range(3, 6)]

            def yn(v, i):
                edge = pltpu.roll(take(ye, step, i), sh_e, 1)
                return jnp.where(lanes == LANES - 1, edge, pltpu.roll(v, LANES - 1, 1))

            def zn(v, i):
                return take(src, i, z + 1)

            def yp(v, i):
                edge = pltpu.roll(take(yh, step, i), sh_h, 1)
                return jnp.where(lanes == 0, edge, pltpu.roll(v, 1, 1))

            def zp(v, i):
                return take(dst, 3 + i, z - 1)

            h = half_h(e, h, dt, (x_next, yn, zn))
            on = jnp.where(z == ZS + 1, 1.0, 0.0)
            e = half_e(e, h, take(fld, 6, z), take(cur) * on, (x_prev, yp, zp))
            for k in range(6):
                v = (tuple(e) + tuple(h))[k]
                at = 0
                for r, n in rows:
                    piece = v[at : at + n]
                    at += n
                    if keep is not None and r in keep:
                        other, first_row, count = keep[r]
                        ri = iota((n, LANES), 0)
                        mine = (ri >= first_row) & (ri < first_row + count)
                        old = other[k, z, pl.ds(r, n), :]
                        piece = jnp.where(mine, piece, old)
                    dst[k, z, pl.ds(r, n), :] = piece

    p4_first = halo_in(0, x_first)
    for c in p_copies:
        c.wait_recv()
    for c in p4_first:
        c.wait_recv()
    build_strips(0)
    for c in s_copies:
        c.wait_recv()
    r8 = iota((8, LANES), 0)

    def tile4(lo, hi):
        return jnp.where(r8 < 3, hi * m_xhi, jnp.where(r8 >= 5, lo * m_xlo, 0.0))

    cur4 = tile4(in_sx[0], in_sx[1])
    cur[pl.ds(CX, 8), :] = cur4
    own4 = pack_s(cur4)
    low32 = (iota((CX, LANES), 1) & 7) < 3
    low8 = (lane & 7) < 3
    own32 = cur_p[pl.ds(0, CX), :]
    src_s[0, pl.ds(0, CX), :] = jnp.where(low32, in_sp[0] * m_ylo, own32)
    src_s[1, pl.ds(0, CX), :] = jnp.where(low32, own32, in_sp[1] * m_yhi)
    src_s[0, pl.ds(CX, 8), :] = jnp.where(low8, tile4(in_sd[0, 0], in_sd[1, 0]) * m_ylo, own4)
    src_s[1, pl.ds(CX, 8), :] = jnp.where(low8, own4, tile4(in_sd[0, 1], in_sd[1, 1]) * m_yhi)

    strips_run()
    plane = ((0, RX),)
    sweep(0, fld, tmp, 6, 11, plane)
    sweep(1, tmp, tmp, 7, 10, plane)
    sweep(2, tmp, tmp, 8, 9, plane)
    own_x = pl.ds(0, CX)
    mine = pl.ds(ring * CX, CX)
    tiles[0, mine, :] = -tmp[4, ZS + 1, own_x, :]
    tiles[1, mine, :] = tmp[3, ZS + 1, own_x, :]
    tiles[2, mine, :] = tmp[1, ZS + 1, own_x, :]
    tiles[3, mine, :] = -tmp[0, ZS + 1, own_x, :]

    def t_copy(d, c, whose):
        at = pl.ds(pl.multiple_of(whose * CX, CX), CX)
        to = lax.rem(ring + d, 8) * 2 + zh
        return remote(
            tiles.at[c, at, :], tiles.at[c, at, :],
            t_send.at[d - 1, c], t_recv.at[d - 1, c], (to, my),
        )

    for c in range(4):
        for d in (4, 3, 5, 2, 6, 1, 7):
            t_copy(d, c, ring).start()
    for c in x_second:
        c.start()

    inner_rows = ((0, CX),)
    sweep(0, fld, tmp, 1, NZ, inner_rows)
    sweep(1, tmp, tmp, 1, NZ, inner_rows)
    sweep(2, tmp, tmp, 1, NZ, inner_rows)

    def store_rows(src, r, n, i):
        return pltpu.make_async_copy(
            src.at[pl.ds(0, 6), pl.ds(1, NZ), pl.ds(r, n), :],
            newf_ref.at[:, :, pl.ds(r, n), :], load_sem.at[i],
        )

    stores = [store_rows(tmp, 8, 16, 2)]
    stores[0].start()

    z_copies = []
    for c in range(4):
        for d in range(1, 8):
            t_copy(d, c, lax.rem(ring + 8 - d, 8)).wait_recv()
        zsend[c, :, :] = jnp.dot(
            weights[...], tiles[c], precision=HI, preferred_element_type=jnp.float32
        )
        copy = remote(zsend.at[c, pl.ds(16, 16), :], zrecv.at[c], z_send.at[c], z_recv.at[c], (partner, my))
        copy.start()
        z_copies.append(copy)

    p4_second = halo_in(1, x_early + x_second)
    for c in p4_second:
        c.wait_recv()
    build_strips(1)
    strips_run()
    outer_rows = ((24, 16), (0, 8))
    sweep(0, fld, fld, 1, NZ, outer_rows)
    sweep(1, fld, fld, 1, NZ, outer_rows)
    sweep(2, fld, fld, 1, NZ, outer_rows, {24: (tmp, 4, 12), 0: (tmp, 0, 4)})
    stores += [store_rows(fld, 0, 8, 3), store_rows(fld, 24, 8, 4)]
    for c in stores[1:]:
        c.start()

    for c in range(4):
        z_copies[c].wait_recv()
        far_ref[pl.ds(c, 16, stride=4), :] = zsend[c, pl.ds(0, 16), :] + zrecv[c]

    @pl.loop(1, NYS)
    def _(d):
        a_copy(d).wait_send()

    for c in x_first + x_early + x_second + p_copies + p4_first + p4_second + s_copies + z_copies:
        c.wait_send()
    for c in range(4):
        for d in range(1, 8):
            t_copy(d, c, ring).wait_send()
    for c in stores:
        c.wait()


def on_device(fields, permittivity, adj_values, adj_owner, adj_row, angle_wave):
    n_adj = adj_values.shape[0]
    f32 = jnp.float32
    vmem = lambda *shape: pltpu.VMEM(shape, f32)
    dma = pltpu.SemaphoreType.DMA
    whole = pl.BlockSpec(memory_space=pltpu.VMEM)
    anywhere = pl.BlockSpec(memory_space=pl.ANY)
    new_fields, far = pl.pallas_call(
        kernel,
        out_shape=(
            jax.ShapeDtypeStruct(fields.shape, f32),
            jax.ShapeDtypeStruct((64, LANES), f32),
        ),
        in_specs=[anywhere, anywhere, whole, whole, whole, whole],
        out_specs=(anywhere, whole),
        scratch_shapes=[
            vmem(7, NZ + 2, RX, LANES),
            vmem(6, NZ + 2, RX, LANES),
            vmem(2, 7, RX, LANES),
            vmem(7, CX, LANES),
            vmem(2, 7, 8, LANES),
            vmem(2, 7, CX, LANES),
            vmem(2, 2, 7, 8, LANES),
            vmem(3, 2, RX, LANES),
            vmem(3, 2, RX, LANES),
            vmem(RX, LANES),
            vmem(2, RX, LANES),
            *[vmem(n, LANES) for _, n in PARTS_LO + PARTS_HI],
            *[vmem(n, LANES) for _, n in PARTS_LO + PARTS_HI],
            vmem(NYS, 8, LANES),
            vmem(NYS, 8, LANES),
            vmem(RX, LANES),
            vmem(RX, LANES),
            vmem(2, 8, LANES),
            vmem(2, CX, LANES),
            vmem(2, 2, 8, LANES),
            vmem(2, RX, LANES),
            vmem(4, 8 * CX, LANES),
            vmem(32, 8 * CX),
            vmem(4, 32, LANES),
            vmem(4, 16, LANES),
            dma((5,)),
            dma((NYS,)),
            dma((NYS,)),
            dma((3, 2)),
            dma((3, 2)),
            dma((2,)),
            dma((2,)),
            dma((2, 2)),
            dma((2, 2)),
            dma((8,)),
            dma((8,)),
            dma((7, 4)),
            dma((7, 4)),
            dma((4,)),
            dma((4,)),
        ],
        compiler_params=pltpu.CompilerParams(collective_id=1, has_side_effects=True),
        name="fdtd_far_field",
    )(
        fields,
        permittivity,
        adj_values,
        adj_owner.reshape(1, n_adj),
        adj_row.reshape(1, n_adj),
        angle_wave.reshape(1, angle_wave.shape[0]),
    )
    return new_fields, far.reshape(8, 2, 4, LANES)


def solution(mesh):
    placed = (
        P(None, None, "xs", "ys"),
        P(None, "xs", "ys"),
        P(("xs", "ys"), None),
        P(("xs", "ys"), None),
        P(("xs", "ys")),
        P(),
    )
    return jax.shard_map(
        on_device,
        mesh=mesh,
        in_specs=placed,
        out_specs=(P(None, None, "xs", "ys"), P("xs", None, None, "ys")),
        check_vma=False,
    )
```

```python
import math

import jax
import jax.numpy as jnp
from jax import lax
from jax.experimental import pallas as pl
from jax.experimental.pallas import tpu as pltpu
from jax.sharding import PartitionSpec as P

GRID_X = 5000
X0 = 2000
ZS = 8
DT = 0.5
NXS = 16
NYS = 48
NZ = 16
CX = 32
RX = 40
LANES = 128
HI = lax.Precision.HIGHEST

FROM_PREV = (
    [(k, r) for k in (0, 1, 2, 4, 5) for r in (29, 30, 31)]
    + [(3, 30), (3, 31)]
    + [(6, 30), (6, 31)]
)
FROM_NEXT = (
    [(k, r) for k in (1, 2) for r in (0, 1, 2)]
    + [(k, r) for k in (0, 3, 4, 5) for r in (0, 1)]
    + [(6, 0), (6, 1)]
)
ALL = tuple(range(7))
EARLY = 2


def split_halo(slabs, boxes):
    inner = {(k, r): (z, n) for comps, r, z, n in boxes for k in comps}
    tile = [(k, r, z, n) for (k, r), (z, n) in inner.items()]
    outer = ([], [])
    for i, (k, r) in enumerate(slabs):
        z, n = inner.get((k, r), (NZ, 0))
        outer[i >= EARLY].append((k, r, 0, z))
        if z + n < NZ:
            outer[i >= EARLY].append((k, r, z + n, NZ - z - n))
    parts = []
    for entries in (tile, *outer):
        placed, at = [], 0
        for k, r, z, n in entries:
            placed.append((k, r, z, n, at))
            at += n
        parts.append((placed, at))
    return parts


PARTS_LO = split_halo(FROM_PREV, ((ALL, 31, 6, 5), (ALL, 30, 7, 3), ((0, 1, 5), 29, 8, 1)))
PARTS_HI = split_halo(FROM_NEXT, ((ALL, 0, 5, 6), (ALL, 1, 6, 4), ((1, 2), 2, 7, 2)))


def iota(shape, axis):
    return lax.broadcasted_iota(jnp.int32, shape, axis)


def half_h(e, h, dt, ops):
    ex, ey, ez = e
    hx, hy, hz = h
    xn, yn, zn = ops
    hx2 = hx - dt * ((yn(ez, 1) - ez) - (zn(ey, 1) - ey))
    hy2 = hy - dt * ((zn(ex, 0) - ex) - (xn(ez) - ez))
    hz2 = hz - dt * ((xn(ey) - ey) - (yn(ex, 0) - ex))
    return hx2, hy2, hz2


def half_e(e, h, c, source, ops):
    ex, ey, ez = e
    hx, hy, hz = h
    xp, yp, zp = ops
    ex2 = ex + c * ((hz - yp(hz, 1)) - (hy - zp(hy, 1)))
    ey2 = ey + c * ((hx - zp(hx, 0)) - (hz - xp(hz)))
    ez2 = ez + c * ((hy - xp(hy)) - (hx - yp(hx, 0)) - source)
    return ex2, ey2, ez2


def kernel(
    fields_ref, perm_ref, adj_ref, owner_ref, row_ref, angle_ref,
    newf_ref, far_ref,
    fld, tmp, strip, own_p, own_p4, in_p, in_p4, ye, yh, dtf, dts,
    send_lo0, send_lo1, send_lo2, send_hi0, send_hi1, send_hi2,
    recv_lo0, recv_lo1, recv_lo2, recv_hi0, recv_hi1, recv_hi2,
    outbox, inbox, cur, cur_p, in_sx, in_sp, in_sd, src_s,
    tiles, weights, zsend, zrecv,
    load_sem, a_send, a_recv, x_send, x_recv, p_send, p_recv, p4_send, p4_recv,
    s_send, s_recv, t_send, t_recv, z_send, z_recv,
):
    send_lo, send_hi = (send_lo0, send_lo1, send_lo2), (send_hi0, send_hi1, send_hi2)
    recv_lo, recv_hi = (recv_lo0, recv_lo1, recv_lo2), (recv_hi0, recv_hi1, recv_hi2)
    mx = lax.axis_index("xs")
    my = lax.axis_index("ys")
    xn_dev = lax.rem(mx + 1, NXS)
    xp_dev = lax.rem(mx + NXS - 1, NXS)
    yn_dev = lax.rem(my + 1, NYS)
    yp_dev = lax.rem(my + NYS - 1, NYS)
    ring = mx // 2
    zh = lax.rem(mx, 2)
    partner = ring * 2 + (1 - zh)
    m_xlo = jnp.where(mx == 0, 0.0, 1.0)
    m_xhi = jnp.where(mx == NXS - 1, 0.0, 1.0)
    m_ylo = jnp.where(my == 0, 0.0, 1.0)
    m_yhi = jnp.where(my == NYS - 1, 0.0, 1.0)

    def remote(src, dst, ssem, rsem, dev):
        return pltpu.make_async_remote_copy(
            src_ref=src, dst_ref=dst, send_sem=ssem, recv_sem=rsem,
            device_id=dev, device_id_type=pl.DeviceIdType.MESH,
        )

    inbox[...] = jnp.zeros(inbox.shape, jnp.float32)
    bar = pltpu.get_barrier_semaphore()

    def greet(dev):
        pl.semaphore_signal(bar, inc=1, device_id=dev, device_id_type=pl.DeviceIdType.MESH)

    near = [
        (xn_dev, my), (xp_dev, my),
        (xn_dev, yn_dev), (xn_dev, yp_dev), (xp_dev, yn_dev), (xp_dev, yp_dev),
    ] + [(lax.rem(ring + d, 8) * 2 + zh, my) for d in range(1, 8)]
    for dev in near:
        greet(dev)

    @pl.loop(1, NYS)
    def _(d):
        greet((mx, lax.rem(my + d, NYS)))

    load_f = pltpu.make_async_copy(
        fields_ref, fld.at[pl.ds(0, 6), pl.ds(1, NZ), pl.ds(0, CX), :], load_sem.at[0]
    )
    load_c = pltpu.make_async_copy(
        perm_ref, fld.at[6, pl.ds(1, NZ), pl.ds(0, CX), :], load_sem.at[1]
    )
    load_f.start()
    load_c.start()

    n_adj = adj_ref.shape[0]
    own_row = owner_ref[...].astype(jnp.float32)
    ii = iota((n_adj, n_adj), 0)
    jj = iota((n_adj, n_adj), 1)
    own_b = jnp.broadcast_to(own_row, (n_adj, n_adj))
    row_b = jnp.broadcast_to(row_ref[...].astype(jnp.float32), (n_adj, n_adj))
    own_col = jnp.sum(jnp.where(ii == jj, own_b, 0.0), axis=1, keepdims=True)
    row_col = jnp.sum(jnp.where(ii == jj, row_b, 0.0), axis=1, keepdims=True)
    same = own_col == own_b
    rank_row = jnp.sum(jnp.where(same & (ii < jj), 1.0, 0.0), axis=0, keepdims=True)
    rank_col = jnp.sum(jnp.where(same & (jj < ii), 1.0, 0.0), axis=1, keepdims=True)
    place = iota((NYS * 8, n_adj), 0).astype(jnp.float32)
    pick_val = jnp.where(place == own_row * 8.0 + rank_row, 1.0, 0.0)
    pick_row = jnp.where(place == own_row * 8.0 + 4.0, 1.0, 0.0)
    lane_f = iota((n_adj, LANES), 1).astype(jnp.float32)
    base = (lax.rem(my, 16) * 8).astype(jnp.float32)
    row_at = jnp.where(lane_f == base + rank_col, row_col + 1.0, 0.0)
    out = jnp.dot(pick_val, adj_ref[...], precision=HI, preferred_element_type=jnp.float32)
    out = out + jnp.dot(pick_row, row_at, precision=HI, preferred_element_type=jnp.float32)
    outbox[...] = out.reshape(NYS, 8, LANES)

    lane = iota((8, LANES), 1)
    for k in range(7):
        for z in range(NZ + 2):
            fld[k, z, pl.ds(CX, 8), :] = jnp.zeros((8, LANES), jnp.float32)
        for z in (0, NZ + 1):
            fld[k, z, pl.ds(0, CX), :] = jnp.zeros((CX, LANES), jnp.float32)
    for k, z in ((3, 5), (4, 5), (3, 0), (4, 0), (0, NZ + 1), (1, NZ + 1)):
        tmp[k, z, :, :] = jnp.zeros((RX, LANES), jnp.float32)
    r40 = iota((RX, LANES), 0)
    row_m = jnp.where(
        r40 < CX, 1.0, jnp.where(r40 < CX + 3, m_xhi, jnp.where(r40 >= RX - 3, m_xlo, 0.0))
    )
    dtf[...] = DT * row_m
    slot40 = iota((RX, LANES), 1) & 7
    dts[0] = DT * row_m * jnp.where(slot40 < 3, m_ylo, jnp.where(slot40 < 6, 1.0, 0.0))
    dts[1] = DT * row_m * jnp.where(slot40 < 3, 1.0, jnp.where(slot40 < 6, m_yhi, 0.0))

    load_f.wait()
    load_c.wait()

    @pl.loop(1, NZ + 1)
    def _(z):
        fld[6, z, pl.ds(0, CX), :] = DT / fld[6, z, pl.ds(0, CX), :]

    flat = fld.reshape(7 * (NZ + 2) * RX, LANES)

    def rows_at(k, z, r, n):
        return pl.ds((k * (NZ + 2) + z + 1) * RX + r, n, stride=RX)

    for sends, parts in ((send_lo, PARTS_LO), (send_hi, PARTS_HI)):
        for send, (entries, _) in zip(sends, parts):
            for k, r, z, n, at in entries:
                send[pl.ds(at, n), :] = flat[rows_at(k, z, r, n), :]

    def pack_strip(load, n):
        lanes = iota((n, LANES), 1)
        total = jnp.zeros((n, LANES), jnp.float32)
        for z in range(NZ):
            turned = pltpu.roll(load(z), 8 * z + 3, 1)
            total = jnp.where((lanes >> 3) == z, turned, total)
        return jnp.where((lanes & 7) < 6, total, 0.0)

    @pl.loop(0, 7)
    def _(k):
        own_p[k, :, :] = pack_strip(lambda z: fld[k, z + 1, pl.ds(0, CX), :], CX)

    r32 = iota((32, LANES), 0)
    owner_xs = jnp.where(r32 < 16, ring * 2 + zh, ring * 2 + (1 - zh))
    a_index = owner_xs * 8 + ((r32 & 15) >> 1)
    angle_row = jnp.broadcast_to(angle_ref[...].astype(jnp.float32), (32, LANES))
    wave = jnp.sum(
        jnp.where(iota((32, LANES), 1) == a_index, angle_row, 0.0), axis=1, keepdims=True
    )
    col = iota((32, 8 * CX), 1)
    x_pos = ((col >> 5) * 2 + zh) * CX + (col & 31) + X0
    prod = wave * x_pos.astype(jnp.float32)
    turn = prod - jnp.floor(prod * (1.0 / GRID_X)) * float(GRID_X)
    turn = jnp.where(turn < 0.0, turn + float(GRID_X), turn)
    turn = jnp.where(turn >= float(GRID_X), turn - float(GRID_X), turn)
    quad = jnp.floor(turn * (4.0 / GRID_X) + 0.5)
    th = (turn - quad * (GRID_X / 4.0)) * (2.0 * math.pi / GRID_X)
    t2 = th * th
    sn = th * (1.0 + t2 * (-1.0 / 6 + t2 * (1.0 / 120 + t2 * (-1.0 / 5040 + t2 * (1.0 / 362880)))))
    cs = 1.0 + t2 * (-0.5 + t2 * (1.0 / 24 + t2 * (-1.0 / 720 + t2 * (1.0 / 40320 - t2 * (1.0 / 3628800)))))
    odd = (quad == 1.0) | (quad == 3.0)
    c_abs = jnp.where(odd, sn, cs)
    s_abs = jnp.where(odd, cs, sn)
    cosine = jnp.where((quad == 1.0) | (quad == 2.0), -c_abs, c_abs)
    sine = jnp.where((quad == 2.0) | (quad == 3.0), -s_abs, s_abs)
    scale = 1.0 / math.sqrt(NXS * CX)
    is_re = (iota((32, 8 * CX), 0) & 1) == 0
    weights[...] = jnp.where(is_re, cosine, -sine) * scale

    pl.semaphore_wait(bar, len(near) + NYS - 1)

    def a_copy(d):
        to = lax.rem(my + d, NYS)
        return remote(
            outbox.at[to, pl.ds(0, 5), :], inbox.at[my, pl.ds(0, 5), :],
            a_send.at[d], a_recv.at[my], (mx, to),
        )

    @pl.loop(1, NYS)
    def _(d):
        a_copy(d).start()

    def x_copies(i):
        return [
            remote(send_lo[i], recv_lo[i], x_send.at[i, 0], x_recv.at[i, 0], (xn_dev, my)),
            remote(send_hi[i], recv_hi[i], x_send.at[i, 1], x_recv.at[i, 1], (xp_dev, my)),
        ]

    x_first, x_early, x_second = x_copies(0), x_copies(1), x_copies(2)
    for c in x_first:
        c.start()
    p_copies = [
        remote(own_p, in_p.at[0], p_send.at[0], p_recv.at[0], (mx, yn_dev)),
        remote(own_p, in_p.at[1], p_send.at[1], p_recv.at[1], (mx, yp_dev)),
    ]
    for c in p_copies + x_early:
        c.start()

    inbox[my] = outbox[my]

    @pl.loop(1, NYS)
    def _(d):
        frm = lax.rem(my + d, NYS)
        remote(
            outbox.at[frm, pl.ds(0, 5), :], inbox.at[frm, pl.ds(0, 5), :],
            a_send.at[d], a_recv.at[frm], (mx, frm),
        ).wait_recv()

    current = jnp.zeros((CX, LANES), jnp.float32)
    x_id = (iota((CX, LANES), 0) + 1).astype(jnp.float32)
    for q in range(3):
        block = inbox[pl.ds(16 * q, 16), :, :]
        ids = jnp.sum(inbox[pl.ds(16 * q, 16), 4, :], axis=0, keepdims=True)
        landing = jnp.where(x_id == ids, 1.0, 0.0)
        current = current + jnp.dot(
            landing, block.reshape(16 * 8, LANES), precision=HI, preferred_element_type=jnp.float32
        )
    cur[pl.ds(0, CX), :] = current

    def pack_s(v):
        lanes = iota(v.shape, 1)
        inside = (lanes >= 8 * ZS) & (lanes < 8 * ZS + 6)
        return jnp.where(inside, pltpu.roll(v, 8 * ZS + 3, 1), 0.0)

    cur_p[pl.ds(0, CX), :] = pack_s(current)
    lo8 = pl.ds(0, 8)
    hi8 = pl.ds(CX - 8, 8)
    s_copies = [
        remote(cur.at[hi8, :], in_sx.at[0], s_send.at[0], s_recv.at[0], (xn_dev, my)),
        remote(cur.at[lo8, :], in_sx.at[1], s_send.at[1], s_recv.at[1], (xp_dev, my)),
        remote(cur_p.at[hi8, :], in_sd.at[0, 0], s_send.at[2], s_recv.at[2], (xn_dev, yn_dev)),
        remote(cur_p.at[hi8, :], in_sd.at[0, 1], s_send.at[3], s_recv.at[3], (xn_dev, yp_dev)),
        remote(cur_p.at[lo8, :], in_sd.at[1, 0], s_send.at[4], s_recv.at[4], (xp_dev, yn_dev)),
        remote(cur_p.at[lo8, :], in_sd.at[1, 1], s_send.at[5], s_recv.at[5], (xp_dev, yp_dev)),
        remote(cur_p.at[pl.ds(0, CX), :], in_sp.at[0], s_send.at[6], s_recv.at[6], (mx, yn_dev)),
        remote(cur_p.at[pl.ds(0, CX), :], in_sp.at[1], s_send.at[7], s_recv.at[7], (mx, yp_dev)),
    ]
    for c in s_copies:
        c.start()

    def unpack_x(i):
        for recv, parts, base, mask in (
            (recv_lo, PARTS_LO, 8, m_xlo), (recv_hi, PARTS_HI, CX, m_xhi)
        ):
            for k, r, z, n, at in parts[i][0]:
                flat[rows_at(k, z, r + base, n), :] = recv[i][pl.ds(at, n), :] * mask

    def p4_copies(part):
        return [
            remote(own_p4.at[part], in_p4.at[part, 0], p4_send.at[part, 0], p4_recv.at[part, 0], (mx, yn_dev)),
            remote(own_p4.at[part], in_p4.at[part, 1], p4_send.at[part, 1], p4_recv.at[part, 1], (mx, yp_dev)),
        ]

    def halo_in(part, copies):
        for c in copies:
            c.wait_recv()
        for i in (0,) if part == 0 else (1, 2):
            unpack_x(i)

        @pl.loop(0, 7)
        def _(k):
            own_p4[part, k, :, :] = pack_strip(lambda z: fld[k, z + 1, pl.ds(CX, 8), :], 8)

        sent = p4_copies(part)
        for c in sent:
            c.start()
        return sent

    def build_strips(part):
        @pl.loop(0, 7)
        def _(k):
            for rows, own, got in (
                (pl.ds(0, CX), own_p[k], (in_p[0, k], in_p[1, k])),
                (pl.ds(CX, 8), own_p4[part, k], (in_p4[part, 0, k], in_p4[part, 1, k])),
            ):
                low = (iota(own.shape, 1) & 7) < 3
                strip[0, k, rows, :] = jnp.where(low, got[0] * m_ylo, own)
                strip[1, k, rows, :] = jnp.where(low, own, got[1] * m_yhi)

    lane40 = iota((RX, LANES), 1)

    def x_next(v):
        return pltpu.roll(v, RX - 1, 0)

    def x_prev(v):
        return pltpu.roll(v, 1, 0)

    def strips_run():
        def zn(v, _):
            return jnp.where(lane40 < 8 * (NZ - 1), pltpu.roll(v, LANES - 8, 1), 0.0)

        def zp(v, _):
            return jnp.where(lane40 >= 8, pltpu.roll(v, 8, 1), 0.0)

        def yn(v, _):
            return pltpu.roll(v, LANES - 1, 1)

        def yp(v, _):
            return pltpu.roll(v, 1, 1)

        for step in range(3):
            for side in range(2):
                e = [strip[side, k] for k in range(3)]
                if side == 1:
                    ye[step, 0, :, :] = e[0]
                    ye[step, 1, :, :] = e[2]
                    if step == 2:
                        continue
                h = [strip[side, k] for k in range(3, 6)]
                h = half_h(e, h, dts[side], (x_next, yn, zn))
                if side == 0:
                    yh[step, 0, :, :] = h[0]
                    yh[step, 1, :, :] = h[2]
                    if step == 2:
                        continue
                e = half_e(e, h, strip[side, 6], src_s[side], (x_prev, yp, zp))
                for k in range(3):
                    strip[side, k, :, :] = e[k]
                    strip[side, 3 + k, :, :] = h[k]

    def sweep(step, src, dst, first, last, rows, keep=None):
        height = sum(n for _, n in rows)
        lanes = iota((height, LANES), 1)

        def take(ref, *at):
            got = [ref[(*at, pl.ds(r, n), slice(None))] for r, n in rows]
            return got[0] if len(got) == 1 else jnp.concatenate(got, axis=0)

        def x_next(v):
            return pltpu.roll(v, height - 1, 0)

        def x_prev(v):
            return pltpu.roll(v, 1, 0)

        @pl.loop(first, last + 1)
        def _(z):
            sh_e = lax.rem(124 - 8 * (z - 1) + 128, 128)
            sh_h = lax.rem(126 - 8 * (z - 1) + 128, 128)
            dt = take(dtf)
            e = [take(src, k, z) for k in range(3)]
            h = [take(src, k, z) for k in range(3, 6)]

            def yn(v, i):
                edge = pltpu.roll(take(ye, step, i), sh_e, 1)
                return jnp.where(lanes == LANES - 1, edge, pltpu.roll(v, LANES - 1, 1))

            def zn(v, i):
                return take(src, i, z + 1)

            def yp(v, i):
                edge = pltpu.roll(take(yh, step, i), sh_h, 1)
                return jnp.where(lanes == 0, edge, pltpu.roll(v, 1, 1))

            def zp(v, i):
                return take(dst, 3 + i, z - 1)

            h = half_h(e, h, dt, (x_next, yn, zn))
            on = jnp.where(z == ZS + 1, 1.0, 0.0)
            e = half_e(e, h, take(fld, 6, z), take(cur) * on, (x_prev, yp, zp))
            for k in range(6):
                v = (tuple(e) + tuple(h))[k]
                at = 0
                for r, n in rows:
                    piece = v[at : at + n]
                    at += n
                    if keep is not None and r in keep:
                        other, first_row, count = keep[r]
                        ri = iota((n, LANES), 0)
                        mine = (ri >= first_row) & (ri < first_row + count)
                        old = other[k, z, pl.ds(r, n), :]
                        piece = jnp.where(mine, piece, old)
                    dst[k, z, pl.ds(r, n), :] = piece

    p4_first = halo_in(0, x_first)
    for c in p_copies:
        c.wait_recv()
    for c in p4_first:
        c.wait_recv()
    build_strips(0)
    for c in s_copies:
        c.wait_recv()
    r8 = iota((8, LANES), 0)

    def tile4(lo, hi):
        return jnp.where(r8 < 3, hi * m_xhi, jnp.where(r8 >= 5, lo * m_xlo, 0.0))

    cur4 = tile4(in_sx[0], in_sx[1])
    cur[pl.ds(CX, 8), :] = cur4
    own4 = pack_s(cur4)
    low32 = (iota((CX, LANES), 1) & 7) < 3
    low8 = (lane & 7) < 3
    own32 = cur_p[pl.ds(0, CX), :]
    src_s[0, pl.ds(0, CX), :] = jnp.where(low32, in_sp[0] * m_ylo, own32)
    src_s[1, pl.ds(0, CX), :] = jnp.where(low32, own32, in_sp[1] * m_yhi)
    src_s[0, pl.ds(CX, 8), :] = jnp.where(low8, tile4(in_sd[0, 0], in_sd[1, 0]) * m_ylo, own4)
    src_s[1, pl.ds(CX, 8), :] = jnp.where(low8, own4, tile4(in_sd[0, 1], in_sd[1, 1]) * m_yhi)

    strips_run()
    plane = ((0, RX),)
    sweep(0, fld, tmp, 6, 11, plane)
    sweep(1, tmp, tmp, 7, 10, plane)
    sweep(2, tmp, tmp, 8, 9, plane)
    own_x = pl.ds(0, CX)
    mine = pl.ds(ring * CX, CX)
    tiles[0, mine, :] = -tmp[4, ZS + 1, own_x, :]
    tiles[1, mine, :] = tmp[3, ZS + 1, own_x, :]
    tiles[2, mine, :] = tmp[1, ZS + 1, own_x, :]
    tiles[3, mine, :] = -tmp[0, ZS + 1, own_x, :]

    def t_copy(d, c, whose):
        at = pl.ds(pl.multiple_of(whose * CX, CX), CX)
        to = lax.rem(ring + d, 8) * 2 + zh
        return remote(
            tiles.at[c, at, :], tiles.at[c, at, :],
            t_send.at[d - 1, c], t_recv.at[d - 1, c], (to, my),
        )

    for c in range(4):
        for d in (4, 3, 5, 2, 6, 1, 7):
            t_copy(d, c, ring).start()
        if c >= 2:
            x_second[c - 2].start()

    inner_rows = ((0, CX),)
    sweep(0, fld, tmp, 1, NZ, inner_rows)
    sweep(1, tmp, tmp, 1, NZ, inner_rows)
    sweep(2, tmp, tmp, 1, NZ, inner_rows)

    def store_rows(src, r, n, i):
        return pltpu.make_async_copy(
            src.at[pl.ds(0, 6), pl.ds(1, NZ), pl.ds(r, n), :],
            newf_ref.at[:, :, pl.ds(r, n), :], load_sem.at[i],
        )

    stores = [store_rows(tmp, 8, 16, 2)]
    stores[0].start()

    z_copies = []
    for c in range(4):
        for d in range(1, 8):
            t_copy(d, c, lax.rem(ring + 8 - d, 8)).wait_recv()
        zsend[c, :, :] = jnp.dot(
            weights[...], tiles[c], precision=HI, preferred_element_type=jnp.float32
        )
        copy = remote(zsend.at[c, pl.ds(16, 16), :], zrecv.at[c], z_send.at[c], z_recv.at[c], (partner, my))
        copy.start()
        z_copies.append(copy)

    p4_second = halo_in(1, x_early + x_second)
    for c in p4_second:
        c.wait_recv()
    build_strips(1)
    strips_run()
    outer_rows = ((24, 16), (0, 8))
    sweep(0, fld, fld, 1, NZ, outer_rows)
    sweep(1, fld, fld, 1, NZ, outer_rows)
    sweep(2, fld, fld, 1, NZ, outer_rows, {24: (tmp, 4, 12), 0: (tmp, 0, 4)})
    stores += [store_rows(fld, 0, 8, 3), store_rows(fld, 24, 8, 4)]
    for c in stores[1:]:
        c.start()

    for c in range(4):
        z_copies[c].wait_recv()
        far_ref[pl.ds(c, 16, stride=4), :] = zsend[c, pl.ds(0, 16), :] + zrecv[c]

    @pl.loop(1, NYS)
    def _(d):
        a_copy(d).wait_send()

    for c in x_first + x_early + x_second + p_copies + p4_first + p4_second + s_copies + z_copies:
        c.wait_send()
    for c in range(4):
        for d in range(1, 8):
            t_copy(d, c, ring).wait_send()
    for c in stores:
        c.wait()


def on_device(fields, permittivity, adj_values, adj_owner, adj_row, angle_wave):
    n_adj = adj_values.shape[0]
    f32 = jnp.float32
    vmem = lambda *shape: pltpu.VMEM(shape, f32)
    dma = pltpu.SemaphoreType.DMA
    whole = pl.BlockSpec(memory_space=pltpu.VMEM)
    anywhere = pl.BlockSpec(memory_space=pl.ANY)
    new_fields, far = pl.pallas_call(
        kernel,
        out_shape=(
            jax.ShapeDtypeStruct(fields.shape, f32),
            jax.ShapeDtypeStruct((64, LANES), f32),
        ),
        in_specs=[anywhere, anywhere, whole, whole, whole, whole],
        out_specs=(anywhere, whole),
        scratch_shapes=[
            vmem(7, NZ + 2, RX, LANES),
            vmem(6, NZ + 2, RX, LANES),
            vmem(2, 7, RX, LANES),
            vmem(7, CX, LANES),
            vmem(2, 7, 8, LANES),
            vmem(2, 7, CX, LANES),
            vmem(2, 2, 7, 8, LANES),
            vmem(3, 2, RX, LANES),
            vmem(3, 2, RX, LANES),
            vmem(RX, LANES),
            vmem(2, RX, LANES),
            *[vmem(n, LANES) for _, n in PARTS_LO + PARTS_HI],
            *[vmem(n, LANES) for _, n in PARTS_LO + PARTS_HI],
            vmem(NYS, 8, LANES),
            vmem(NYS, 8, LANES),
            vmem(RX, LANES),
            vmem(RX, LANES),
            vmem(2, 8, LANES),
            vmem(2, CX, LANES),
            vmem(2, 2, 8, LANES),
            vmem(2, RX, LANES),
            vmem(4, 8 * CX, LANES),
            vmem(32, 8 * CX),
            vmem(4, 32, LANES),
            vmem(4, 16, LANES),
            dma((5,)),
            dma((NYS,)),
            dma((NYS,)),
            dma((3, 2)),
            dma((3, 2)),
            dma((2,)),
            dma((2,)),
            dma((2, 2)),
            dma((2, 2)),
            dma((8,)),
            dma((8,)),
            dma((7, 4)),
            dma((7, 4)),
            dma((4,)),
            dma((4,)),
        ],
        compiler_params=pltpu.CompilerParams(collective_id=1, has_side_effects=True),
        name="fdtd_far_field",
    )(
        fields,
        permittivity,
        adj_values,
        adj_owner.reshape(1, n_adj),
        adj_row.reshape(1, n_adj),
        angle_wave.reshape(1, angle_wave.shape[0]),
    )
    return new_fields, far.reshape(8, 2, 4, LANES)


def solution(mesh):
    placed = (
        P(None, None, "xs", "ys"),
        P(None, "xs", "ys"),
        P(("xs", "ys"), None),
        P(("xs", "ys"), None),
        P(("xs", "ys")),
        P(),
    )
    return jax.shard_map(
        on_device,
        mesh=mesh,
        in_specs=placed,
        out_specs=(P(None, None, "xs", "ys"), P("xs", None, None, "ys")),
        check_vma=False,
    )
```
